32 devices in a mesh: region: 2 (over y), tile: 4 (over z), shot: 2 (over x), pair: 2 (over core).
Axes of the slice: x: 2, y: 2, z: 4, core: 2. Of those that a mesh axis runs over, the one named last changes fastest.
Arguments:
- velocity: float32 [64, 128, 128], P(('region', 'tile'), ('shot', 'pair')), parts along dimension 0, may hold values from 1.5 to 4.5
- anchors: int32 [4], P(('region', 'shot')), parts along dimension 0, may hold values from 0 to 64, as said below
- source_prev: float32 [8, 32, 64, 128], P(('region', 'shot', 'pair'), 'tile'), parts along dimension 0, may hold values from -6 to 6
- source_now: float32 [8, 32, 64, 128], P(('region', 'shot', 'pair'), 'tile'), parts along dimension 0, may hold values from -6 to 6
- recv_prev: float32 [8, 32, 64, 128], P(('region', 'shot', 'pair'), 'tile'), parts along dimension 0, may hold values from -6 to 6
- recv_now: float32 [8, 32, 64, 128], P(('region', 'shot', 'pair'), 'tile'), parts along dimension 0, may hold values from -6 to 6
- source_x: int32 [8], P(('region', 'shot', 'pair')), parts along dimension 0, may hold values from 0 to 31
- source_yz: int32 [8], P(('region', 'shot', 'pair')), parts along dimension 0, may hold values from 0 to 8191
- wavelet: float32 [8, 6], P(('region', 'shot', 'pair')), parts along dimension 0, may hold values from -6 to 6
- recv_x: int32 [8, 128], P(('region', 'shot', 'pair')), parts along dimension 0, may hold values from 0 to 31
- recv_yz: int32 [8, 128], P(('region', 'shot', 'pair')), parts along dimension 0, may hold values from 0 to 8191
- record: float32 [8, 6, 128], P(('region', 'shot', 'pair')), parts along dimension 0, may hold values from -6 to 6
Outputs:
- image: float32 [64, 128, 128], P(('region', 'tile'), ('shot', 'pair')), parts along dimension 0
- source_field: float32 [8, 32, 64, 128], P(('region', 'shot', 'pair'), 'tile'), parts along dimension 0
- receiver_field: float32 [8, 32, 64, 128], P(('region', 'shot', 'pair'), 'tile'), parts along dimension 0
The draws below stay inside these ranges and needn't reach their ends.
There are 2 independent parts, one for each index of `region`. The reference program is written for one: setup_inputs(seed, part) draws one part's arguments, and reference() takes and returns one part's arrays. A program takes and returns all parts, laid end to end along the dimension named above; each array names one. Nothing has to cross between parts.
Inputs may be any that keep to these rules, and one draw needn't show every extreme that they name: Aperture a covers survey rows anchors[a] to anchors[a] + 63 along the second dimension; in every draw some aperture starts at 64.
All inputs are finite; a program needn't handle non-finite values.
Results may differ from the reference program's by a relative error of at most 0.00002.
Values sent between devices are 32-bit elements; how exact they have to be, the bound alone decides.
A program may use at most 64 MiB of HBM per device.

```python
import jax
import jax.numpy as jnp
from jax import lax

Z = 128
STEPS = 6
NREC = 128
SHOTS = 4
APERTURES = 2
AX = 32
NYS = 128
AY = 64
N_PAIR = 2


def draw_anchors(key, part):
    highest = NYS - AY
    values = jax.random.randint(jax.random.fold_in(key, 11), (APERTURES,), 0, highest + 1, dtype=jnp.int32)
    chosen = jax.random.randint(jax.random.fold_in(key, 12), (), 0, APERTURES, dtype=jnp.int32)
    places = jnp.arange(APERTURES, dtype=jnp.int32)
    return jnp.where(places == chosen, highest, values).astype(jnp.int32)


def touch_ends(values, rng, smallest, high):
    extent = values.shape
    index_at = [jax.random.randint(jax.random.fold_in(rng, axis), (), 0, extent[axis]) for axis in range(len(extent))]
    values = values.at[tuple(index_at)].set(smallest)
    longest = extent.index(max(extent))
    index_at[longest] = (index_at[longest] + 1) % extent[longest]
    return values.at[tuple(index_at)].set(high)


def block_levels(stream_key, shape, split, low, top_value):
    level, own = 1.0, jax.random.fold_in(stream_key, 6)
    for axis_at, shards_of in split:
        steps = jnp.exp(jax.random.uniform(jax.random.fold_in(own, axis_at), (shards_of,), jnp.float32, low / len(split), top_value / len(split)))
        level = level * jnp.repeat(steps, shape[axis_at] // shards_of).reshape([-1 if axis == axis_at else 1 for axis in range(len(shape))])
    return level


def normal_values(key, extent, scale, bound, pieces=(), kind=jnp.bfloat16):
    loudness = block_levels(key, extent, pieces, -0.22, 0.18) if pieces else 1.0
    result = jax.random.normal(key, extent, jnp.float32) * scale * loudness
    return jnp.minimum(jnp.maximum(result, -bound), bound).astype(kind)


def setup_inputs(seed: int = 0, part: int = 0) -> dict:
    key_list = jax.random.split(jax.random.key(seed), 13)
    part_splits = jax.random.split(jax.random.fold_in(key_list[12], part), 13)
    return {
        "velocity": jnp.clip(1.5 + 3.0 * jax.random.uniform(part_splits[0], (AX, NYS, Z), jnp.float32) ** block_levels(part_splits[0], (AX, NYS, Z), ((0, 4), (1, 4)), -0.2, 0.2), 1.5, 4.5),
        "anchors": draw_anchors(jax.random.fold_in(jax.random.fold_in(key_list[12], part), 71), part),
        "source_prev": normal_values(part_splits[2], (SHOTS, AX, AY, Z), 1.0, 6.0, ((0, 4), (1, 4)), jnp.float32),
        "source_now": normal_values(part_splits[3], (SHOTS, AX, AY, Z), 1.0, 6.0, ((0, 4), (1, 4)), jnp.float32),
        "recv_prev": normal_values(part_splits[4], (SHOTS, AX, AY, Z), 1.0, 6.0, ((0, 4), (1, 4)), jnp.float32),
        "recv_now": normal_values(part_splits[5], (SHOTS, AX, AY, Z), 1.0, 6.0, ((0, 4), (1, 4)), jnp.float32),
        "source_x": touch_ends(jax.random.randint(part_splits[6], (SHOTS,), 0, AX), jax.random.fold_in(part_splits[6], 1), 0, AX - 1).astype(jnp.int32),
        "source_yz": touch_ends(jax.random.randint(part_splits[7], (SHOTS,), 0, AY * Z), jax.random.fold_in(part_splits[7], 1), 0, (AY * Z) - 1).astype(jnp.int32),
        "wavelet": normal_values(part_splits[8], (SHOTS, STEPS), 1.0, 6.0, ((0, 4),), jnp.float32),
        "recv_x": touch_ends(jax.random.randint(part_splits[9], (SHOTS, NREC), 0, AX), jax.random.fold_in(part_splits[9], 1), 0, AX - 1).astype(jnp.int32),
        "recv_yz": touch_ends(jax.random.randint(part_splits[10], (SHOTS, NREC), 0, AY * Z), jax.random.fold_in(part_splits[10], 1), 0, (AY * Z) - 1).astype(jnp.int32),
        "record": normal_values(part_splits[11], (SHOTS, STEPS, NREC), 1.0, 6.0, ((0, 4),), jnp.float32),
    }


stencil_weights = (-205.0 / 72.0, 8.0 / 5.0, -1.0 / 5.0, 8.0 / 315.0, -1.0 / 560.0)
courant_scale = 0.1


def laplace(extended):
    length = extended.shape[1]
    across = extended.shape[2]
    downward = extended.shape[3]
    interior = length - 8
    padded = jnp.pad(extended, ((0, 0), (0, 0), (4, 4), (4, 4)))

    def sample(along_x, along_y, along_z):
        return padded[:, 4 + along_x:4 + along_x + interior, 4 + along_y:4 + along_y + across, 4 + along_z:4 + along_z + downward]

    total = 3.0 * stencil_weights[0] * sample(0, 0, 0)
    for reach in range(1, 5):
        neighbour_sum = sample(reach, 0, 0) + sample(-reach, 0, 0) + sample(0, reach, 0) + sample(0, -reach, 0) + sample(0, 0, reach) + sample(0, 0, -reach)
        total = total + stencil_weights[reach] * neighbour_sum
    return total


def advance(older, current, courant):
    extended = jnp.pad(current, ((0, 0), (4, 4), (0, 0), (0, 0)))
    return 2.0 * current - older + courant * laplace(extended)


def deposit(fields, columns, planes, amounts):
    flat = fields.reshape(SHOTS, AX * AY * Z)
    shot_rows = jnp.zeros_like(columns) + jnp.arange(SHOTS, dtype=jnp.int32)[:, None]
    target = columns * (AY * Z) + planes
    return flat.at[shot_rows, target].add(amounts).reshape(fields.shape)


def reference(velocity, anchors, source_prev, source_now, recv_prev, recv_now, source_x, source_yz, wavelet, recv_x, recv_yz, record):
    starts = anchors.astype(jnp.int32)
    windows = [lax.dynamic_slice_in_dim(velocity, starts[member // N_PAIR], AY, 1) for member in range(SHOTS)]
    scaled = jnp.stack(windows) * courant_scale
    courant = scaled * scaled
    older_source, current_source = source_prev, source_now
    older_receiver, current_receiver = recv_prev, recv_now
    image_shots = jnp.zeros(source_now.shape, jnp.float32)
    for moment in range(STEPS):
        new_source = advance(older_source, current_source, courant)
        new_source = deposit(new_source, source_x[:, None], source_yz[:, None], wavelet[:, moment][:, None])
        new_receiver = advance(older_receiver, current_receiver, courant)
        new_receiver = deposit(new_receiver, recv_x, recv_yz, record[:, moment, :])
        image_shots = image_shots + new_source * new_receiver
        older_source, current_source = current_source, new_source
        older_receiver, current_receiver = current_receiver, new_receiver
    image = jnp.zeros((AX, NYS, Z), jnp.float32)
    for member in range(SHOTS):
        placed = lax.dynamic_update_slice_in_dim(jnp.zeros((AX, NYS, Z), jnp.float32), image_shots[member], starts[member // N_PAIR], 1)
        image = image + placed
    return image, current_source, current_receiver
```

```python
import functools

import jax
import jax.numpy as jnp
from jax import lax
from jax.experimental import pallas as pl
from jax.experimental.pallas import tpu as pltpu
from jax.sharding import PartitionSpec as P

STEPS = 6
MESH = pl.DeviceIdType.MESH

stencil_weights = (-205.0 / 72.0, 8.0 / 5.0, -1.0 / 5.0, 8.0 / 315.0, -1.0 / 560.0)
courant_scale = 0.1

PAD = 8
CHUNKS = 4


def kernel(
    sizes,
    anchors,
    source_x,
    source_yz,
    wavelet,
    recv_x,
    recv_yz,
    record,
    velocity,
    source_prev,
    source_now,
    recv_prev,
    recv_now,
    image_out,
    source_out,
    recv_out,
    field,
    speed,
    courant,
    injected,
    stacked,
    mate_out,
    mate_in,
    shot_out,
    shot_in,
    total,
    load_sem,
    halo_send,
    halo_recv,
    speed_send,
    speed_recv,
    mate_speed_send,
    mate_speed_recv,
    mate_sem,
    shot_send,
    shot_recv,
    out_sem,
):
    n_tile, n_shot, n_pair = sizes
    width, across, downward = source_now.shape[1:]
    owned = velocity.shape[1]
    survey = owned * n_shot * n_pair
    margin = survey - across
    rows = across // CHUNKS
    tile = lax.axis_index("tile")
    shot = lax.axis_index("shot")
    pair = lax.axis_index("pair")
    mate = 1 - pair
    has_low = tile > 0
    has_high = tile < n_tile - 1

    barrier = pltpu.get_barrier_semaphore()

    @pl.when(has_low)
    def _():
        pl.semaphore_signal(barrier, inc=1, device_id={"tile": tile - 1}, device_id_type=MESH)

    @pl.when(has_high)
    def _():
        pl.semaphore_signal(barrier, inc=1, device_id={"tile": tile + 1}, device_id_type=MESH)

    pl.semaphore_signal(barrier, inc=1, device_id={"pair": mate}, device_id_type=MESH)
    for k in range(1, n_shot):
        pl.semaphore_signal(barrier, inc=1, device_id={"shot": lax.rem(shot + k, n_shot)}, device_id_type=MESH)

    def owner_rows(s, p):
        return pl.ds(pl.multiple_of((s * n_pair + p) * owned, owned), owned)

    inner = pl.ds(PAD, across)
    loads = [
        pltpu.make_async_copy(source_now.at[0], field.at[0, 0, 4 : 4 + width, inner], load_sem.at[0]),
        pltpu.make_async_copy(recv_now.at[0], field.at[0, 1, 4 : 4 + width, inner], load_sem.at[1]),
        pltpu.make_async_copy(source_prev.at[0], field.at[1, 0, 4 : 4 + width, inner], load_sem.at[2]),
        pltpu.make_async_copy(recv_prev.at[0], field.at[1, 1, 4 : 4 + width, inner], load_sem.at[3]),
        pltpu.make_async_copy(velocity, speed.at[:, owner_rows(shot, pair)], load_sem.at[4]),
    ]
    for copy in loads:
        copy.start()

    neighbours = n_shot + has_low.astype(jnp.int32) + has_high.astype(jnp.int32)
    pl.semaphore_wait(barrier, neighbours)

    def start_halo(c, f, now):
        part = pl.ds(pl.multiple_of(c * rows, rows), rows)
        landing = pl.ds(pl.multiple_of(PAD + c * rows, 8), rows)

        @pl.when(has_low)
        def _():
            pltpu.make_async_remote_copy(
                now.at[0, 0:4, part],
                field.at[0, f, 4 + width : 8 + width, landing],
                halo_send.at[0, c, 0],
                halo_recv.at[0, c, 1],
                device_id={"tile": tile - 1},
                device_id_type=MESH,
            ).start()

        @pl.when(has_high)
        def _():
            pltpu.make_async_remote_copy(
                now.at[0, width - 4 : width, part],
                field.at[0, f, 0:4, landing],
                halo_send.at[0, c, 1],
                halo_recv.at[0, c, 0],
                device_id={"tile": tile + 1},
                device_id_type=MESH,
            ).start()

    def halo(n, slot, c, side):
        landing = pl.ds(pl.multiple_of(PAD + c * rows, 8), rows)
        if side == 0:
            source, target, other = pl.ds(4, 4), pl.ds(4 + width, 4), tile - 1
        else:
            source, target, other = pl.ds(width, 4), pl.ds(0, 4), tile + 1
        return pltpu.make_async_remote_copy(
            field.at[slot, :, source, landing],
            field.at[slot, :, target, landing],
            halo_send.at[n, c, side],
            halo_recv.at[n, c, 1 - side],
            device_id={"tile": other},
            device_id_type=MESH,
        )

    for k in range(1, n_shot):
        pltpu.make_async_remote_copy(
            velocity,
            speed.at[:, owner_rows(shot, pair)],
            speed_send.at[k],
            speed_recv.at[k],
            device_id={"shot": lax.rem(shot + k, n_shot)},
            device_id_type=MESH,
        ).start()
    pltpu.make_async_remote_copy(
        velocity,
        speed.at[:, owner_rows(shot, pair)],
        mate_speed_send.at[0],
        mate_speed_recv.at[0],
        device_id={"pair": mate},
        device_id_type=MESH,
    ).start()
    for c in range(CHUNKS):
        start_halo(c, 0, source_now)
        start_halo(c, 1, recv_now)

    for slot in range(2):
        for f in range(2):
            field[slot, f, 4 : 4 + width, 0:PAD] = jnp.zeros((width, PAD, downward), jnp.float32)
            field[slot, f, 4 : 4 + width, PAD + across : 2 * PAD + across] = jnp.zeros((width, PAD, downward), jnp.float32)

    def clear(first):
        def body(i, _):
            field[i // 8, (i // 4) % 2, first + i % 4] = jnp.zeros((across + 2 * PAD, downward), jnp.float32)
            return 0

        lax.fori_loop(0, 16, body, 0)

    @pl.when(jnp.logical_not(has_low))
    def _():
        clear(0)

    @pl.when(jnp.logical_not(has_high))
    def _():
        clear(4 + width)

    def clear_image(i, _):
        stacked[i] = jnp.zeros((2 * margin + across, downward), jnp.float32)
        return 0

    lax.fori_loop(0, width, clear_image, 0)

    first = tile * width
    place = (recv_x[...] - first) * across + recv_yz[...] // downward
    depth = recv_yz[...] % downward
    receivers = record.shape[2]
    cell = lax.broadcasted_iota(jnp.int32, (width * across, receivers), 0)
    pick = jnp.where(cell == place, 1.0, 0.0).astype(jnp.bfloat16)
    at_depth = lax.broadcasted_iota(jnp.int32, (downward, receivers), 0) == depth

    def inject(n, _):
        amount = record[0, pl.ds(n, 1), :]
        high = amount.astype(jnp.bfloat16).astype(jnp.float32)
        rest = amount - high
        middle = rest.astype(jnp.bfloat16).astype(jnp.float32)
        low = rest - middle
        dense = jnp.zeros((width * across, downward), jnp.float32)
        for piece in (low, middle, high):
            spread = jnp.where(at_depth, piece, 0.0).astype(jnp.bfloat16)
            dense = dense + lax.dot_general(
                pick, spread, (((1,), (1,)), ((), ())), preferred_element_type=jnp.float32
            )
        injected[n] = dense.reshape(width, across, downward)
        return 0

    lax.fori_loop(0, STEPS, inject, 0)

    for k in range(1, n_shot):
        origin = lax.rem(shot + n_shot - k, n_shot)
        block = speed.at[:, owner_rows(origin, pair)]
        pltpu.make_async_remote_copy(
            velocity, block, speed_send.at[k], speed_recv.at[k], device_id={"pair": mate}, device_id_type=MESH
        ).wait()
        pltpu.make_async_remote_copy(
            block, block, mate_speed_send.at[k], mate_speed_recv.at[k], device_id={"pair": mate}, device_id_type=MESH
        ).start()
    for copy in loads:
        copy.wait()
    for k in range(n_shot):
        origin = lax.rem(shot + n_shot - k, n_shot)
        pltpu.make_async_remote_copy(
            velocity,
            speed.at[:, owner_rows(origin, mate)],
            mate_speed_send.at[k],
            mate_speed_recv.at[k],
            device_id={"pair": mate},
            device_id_type=MESH,
        ).wait()

    start_row = anchors[0]

    def refresh(i, _):
        scaled = speed[i, pl.ds(start_row, across), :] * courant_scale
        courant[i] = scaled * scaled
        return 0

    lax.fori_loop(0, width, refresh, 0)

    lane = lax.broadcasted_iota(jnp.int32, (1, 1, downward), 2)
    behind = [jnp.where(lane >= r, stencil_weights[r], 0.0) for r in range(1, 5)]
    ahead = [jnp.where(lane < downward - r, stencil_weights[r], 0.0) for r in range(1, 5)]
    shape = (width, 8, downward)
    local_cell = (
        lax.broadcasted_iota(jnp.int32, shape, 0) * (across * downward)
        + lax.broadcasted_iota(jnp.int32, shape, 1) * downward
        + lax.broadcasted_iota(jnp.int32, shape, 2)
    )
    source_cell = (source_x[0] - first) * (across * downward) + source_yz[0]

    def update(s, slot, y0):
        at = pl.multiple_of(PAD + y0, 8)
        gain = courant[:, pl.ds(y0, 8), :]
        results = []
        for f in range(2):
            column = field[slot, f, :, pl.ds(at, 8), :]
            centre = column[4 : 4 + width]
            sums = (3.0 * stencil_weights[0]) * centre
            for r in range(1, 5):
                near = column[4 - r : 4 - r + width] + column[4 + r : 4 + r + width]
                near = near + field[slot, f, 4 : 4 + width, pl.ds(at - r, 8), :]
                near = near + field[slot, f, 4 : 4 + width, pl.ds(at + r, 8), :]
                sums = sums + stencil_weights[r] * near
                sums = sums + behind[r - 1] * pltpu.roll(centre, r, 2)
                sums = sums + ahead[r - 1] * pltpu.roll(centre, downward - r, 2)
            older = field[1 - slot, f, 4 : 4 + width, pl.ds(at, 8), :]
            fresh = 2.0 * centre - older + gain * sums
            if f == 0:
                fresh = fresh + jnp.where(local_cell == source_cell - y0 * downward, wavelet[0, s], 0.0)
            else:
                fresh = fresh + injected[s, :, pl.ds(y0, 8), :]
            field[1 - slot, f, 4 : 4 + width, pl.ds(at, 8), :] = fresh
            results.append(fresh)
        spot = pl.ds(pl.multiple_of(margin + y0, 8), 8)
        stacked[:, spot, :] = stacked[:, spot, :] + results[0] * results[1]

    def step(s, _):
        slot = lax.rem(s, 2)

        def chunk(c, _):
            @pl.when(has_low)
            def _():
                halo(s, slot, c, 1).wait_recv()

            @pl.when(has_high)
            def _():
                halo(s, slot, c, 0).wait_recv()

            @pl.when(jnp.logical_and(has_low, s > 0))
            def _():
                halo(s - 1, 1 - slot, c, 0).wait_send()

            @pl.when(jnp.logical_and(has_high, s > 0))
            def _():
                halo(s - 1, 1 - slot, c, 1).wait_send()

            def tiles(t, _):
                update(s, slot, pl.multiple_of(c * rows + t * 8, 8))
                return 0

            lax.fori_loop(0, rows // 8, tiles, 0)

            @pl.when(jnp.logical_and(has_low, s < STEPS - 1))
            def _():
                halo(s + 1, 1 - slot, c, 0).start()

            @pl.when(jnp.logical_and(has_high, s < STEPS - 1))
            def _():
                halo(s + 1, 1 - slot, c, 1).start()

            return 0

        lax.fori_loop(0, CHUNKS, chunk, 0)
        return 0

    lax.fori_loop(0, STEPS, step, 0)

    final = STEPS % 2
    stores = [
        pltpu.make_async_copy(field.at[final, 0, 4 : 4 + width, inner], source_out.at[0], out_sem.at[0]),
        pltpu.make_async_copy(field.at[final, 1, 4 : 4 + width, inner], recv_out.at[0], out_sem.at[1]),
    ]
    for copy in stores:
        copy.start()

    def contribution(s, p):
        return stacked[:, pl.ds((s * n_pair + p) * owned + margin - start_row, owned), :]

    for k in range(n_shot):
        mate_out[k] = contribution(lax.rem(shot + k, n_shot), mate)
        pltpu.make_async_remote_copy(
            mate_out.at[k],
            mate_in.at[k],
            mate_sem.at[0, k],
            mate_sem.at[1, k],
            device_id={"pair": mate},
            device_id_type=MESH,
        ).start()

    def mate_copy(k):
        return pltpu.make_async_remote_copy(
            mate_out.at[k],
            mate_in.at[k],
            mate_sem.at[0, k],
            mate_sem.at[1, k],
            device_id={"pair": mate},
            device_id_type=MESH,
        )

    def shot_copy(k):
        return pltpu.make_async_remote_copy(
            shot_out.at[k - 1],
            shot_in.at[k - 1],
            shot_send.at[k - 1],
            shot_recv.at[k - 1],
            device_id={"shot": lax.rem(shot + k, n_shot)},
            device_id_type=MESH,
        )

    for k in range(1, n_shot):
        mate_copy(k).wait_recv()
        shot_out[k - 1] = contribution(lax.rem(shot + k, n_shot), pair) + mate_in[k]
        shot_copy(k).start()
    mate_copy(0).wait_recv()
    mine = contribution(shot, pair) + mate_in[0]
    for k in range(1, n_shot):
        shot_copy(k).wait_recv()
        mine = mine + shot_in[k - 1]
    total[...] = mine
    last = pltpu.make_async_copy(total, image_out, out_sem.at[2])
    last.start()

    for c in range(CHUNKS):
        @pl.when(has_low)
        def _():
            halo(STEPS - 1, (STEPS - 1) % 2, c, 0).wait_send()

        @pl.when(has_high)
        def _():
            halo(STEPS - 1, (STEPS - 1) % 2, c, 1).wait_send()

    for k in range(n_shot):
        mate_copy(k).wait_send()
    for k in range(1, n_shot):
        shot_copy(k).wait_send()
    for copy in stores:
        copy.wait()
    last.wait()


def solution(mesh):
    sizes = (mesh.shape["tile"], mesh.shape["shot"], mesh.shape["pair"])
    n_shot, n_pair = sizes[1:]

    def shards(velocity, anchors, source_prev, source_now, recv_prev, recv_now, source_x, source_yz, wavelet, recv_x, recv_yz, record):
        width, across, downward = source_now.shape[1:]
        owned = velocity.shape[1]
        survey = owned * n_shot * n_pair
        margin = survey - across
        f32 = jnp.float32
        block = (width, owned, downward)
        smem = pl.BlockSpec(memory_space=pltpu.SMEM)
        vmem = pl.BlockSpec(memory_space=pltpu.VMEM)
        anywhere = pl.BlockSpec(memory_space=pl.ANY)
        dma = pltpu.SemaphoreType.DMA
        return pl.pallas_call(
            functools.partial(kernel, sizes),
            out_shape=(
                jax.ShapeDtypeStruct(velocity.shape, f32),
                jax.ShapeDtypeStruct(source_now.shape, f32),
                jax.ShapeDtypeStruct(recv_now.shape, f32),
            ),
            in_specs=[smem] * 4 + [vmem] * 3 + [anywhere] * 5,
            out_specs=(anywhere,) * 3,
            scratch_shapes=[
                pltpu.VMEM((2, 2, width + 8, across + 2 * PAD, downward), f32),
                pltpu.VMEM((width, survey, downward), f32),
                pltpu.VMEM((width, across, downward), f32),
                pltpu.VMEM((STEPS, width, across, downward), f32),
                pltpu.VMEM((width, across + 2 * margin, downward), f32),
                pltpu.VMEM((n_shot,) + block, f32),
                pltpu.VMEM((n_shot,) + block, f32),
                pltpu.VMEM((n_shot - 1,) + block, f32),
                pltpu.VMEM((n_shot - 1,) + block, f32),
                pltpu.VMEM(block, f32),
                dma((5,)),
                dma((STEPS, CHUNKS, 2)),
                dma((STEPS, CHUNKS, 2)),
                dma((n_shot,)),
                dma((n_shot,)),
                dma((n_shot,)),
                dma((n_shot,)),
                dma((2, n_shot)),
                dma((n_shot - 1,)),
                dma((n_shot - 1,)),
                dma((3,)),
            ],
            compiler_params=pltpu.CompilerParams(
                collective_id=0, has_side_effects=True, vmem_limit_bytes=48 * 1024 * 1024
            ),
        )(anchors, source_x, source_yz, wavelet, recv_x, recv_yz, record, velocity, source_prev, source_now, recv_prev, recv_now)

    in_specs = (
        P(("region", "tile"), ("shot", "pair"), None),
        P(("region", "shot")),
        P(("region", "shot", "pair"), "tile", None, None),
        P(("region", "shot", "pair"), "tile", None, None),
        P(("region", "shot", "pair"), "tile", None, None),
        P(("region", "shot", "pair"), "tile", None, None),
        P(("region", "shot", "pair")),
        P(("region", "shot", "pair")),
        P(("region", "shot", "pair"), None),
        P(("region", "shot", "pair"), None),
        P(("region", "shot", "pair"), None),
        P(("region", "shot", "pair"), None, None),
    )
    out_specs = (
        P(("region", "tile"), ("shot", "pair"), None),
        P(("region", "shot", "pair"), "tile", None, None),
        P(("region", "shot", "pair"), "tile", None, None),
    )
    return jax.shard_map(shards, mesh=mesh, in_specs=in_specs, out_specs=out_specs, check_vma=False)
```

```python
import functools

import jax
import jax.numpy as jnp
from jax import lax
from jax.experimental import pallas as pl
from jax.experimental.pallas import tpu as pltpu
from jax.sharding import PartitionSpec as P

STEPS = 6
MESH = pl.DeviceIdType.MESH

stencil_weights = (-205.0 / 72.0, 8.0 / 5.0, -1.0 / 5.0, 8.0 / 315.0, -1.0 / 560.0)
courant_scale = 0.1

PAD = 8
CHUNKS = 4


def kernel(
    sizes,
    anchors,
    source_x,
    source_yz,
    wavelet,
    recv_x,
    recv_yz,
    record,
    velocity,
    source_prev,
    source_now,
    recv_prev,
    recv_now,
    image_out,
    source_out,
    recv_out,
    field,
    speed,
    courant,
    injected,
    stacked,
    mate_out,
    mate_in,
    shot_out,
    shot_in,
    total,
    load_sem,
    halo_send,
    halo_recv,
    speed_send,
    speed_recv,
    mate_speed_send,
    mate_speed_recv,
    mate_sem,
    shot_send,
    shot_recv,
    out_sem,
):
    n_tile, n_shot, n_pair = sizes
    width, across, downward = source_now.shape[1:]
    owned = velocity.shape[1]
    survey = owned * n_shot * n_pair
    margin = survey - across
    rows = across // CHUNKS
    tile = lax.axis_index("tile")
    shot = lax.axis_index("shot")
    pair = lax.axis_index("pair")
    mate = 1 - pair
    has_low = tile > 0
    has_high = tile < n_tile - 1

    barrier = pltpu.get_barrier_semaphore()

    @pl.when(has_low)
    def _():
        pl.semaphore_signal(barrier, inc=1, device_id={"tile": tile - 1}, device_id_type=MESH)

    @pl.when(has_high)
    def _():
        pl.semaphore_signal(barrier, inc=1, device_id={"tile": tile + 1}, device_id_type=MESH)

    pl.semaphore_signal(barrier, inc=1, device_id={"pair": mate}, device_id_type=MESH)
    for k in range(1, n_shot):
        pl.semaphore_signal(barrier, inc=1, device_id={"shot": lax.rem(shot + k, n_shot)}, device_id_type=MESH)

    def owner_rows(s, p):
        return pl.ds(pl.multiple_of((s * n_pair + p) * owned, owned), owned)

    inner = pl.ds(PAD, across)
    loads = [
        pltpu.make_async_copy(source_now.at[0], field.at[0, 0, 4 : 4 + width, inner], load_sem.at[0]),
        pltpu.make_async_copy(recv_now.at[0], field.at[0, 1, 4 : 4 + width, inner], load_sem.at[1]),
        pltpu.make_async_copy(source_prev.at[0], field.at[1, 0, 4 : 4 + width, inner], load_sem.at[2]),
        pltpu.make_async_copy(recv_prev.at[0], field.at[1, 1, 4 : 4 + width, inner], load_sem.at[3]),
        pltpu.make_async_copy(velocity, speed.at[:, owner_rows(shot, pair)], load_sem.at[4]),
    ]
    for copy in loads:
        copy.start()

    neighbours = n_shot + has_low.astype(jnp.int32) + has_high.astype(jnp.int32)
    pl.semaphore_wait(barrier, neighbours)

    def start_halo(c, f, now):
        part = pl.ds(pl.multiple_of(c * rows, rows), rows)
        landing = pl.ds(pl.multiple_of(PAD + c * rows, 8), rows)

        @pl.when(has_low)
        def _():
            pltpu.make_async_remote_copy(
                now.at[0, 0:4, part],
                field.at[0, f, 4 + width : 8 + width, landing],
                halo_send.at[0, c, 0],
                halo_recv.at[0, c, 1],
                device_id={"tile": tile - 1},
                device_id_type=MESH,
            ).start()

        @pl.when(has_high)
        def _():
            pltpu.make_async_remote_copy(
                now.at[0, width - 4 : width, part],
                field.at[0, f, 0:4, landing],
                halo_send.at[0, c, 1],
                halo_recv.at[0, c, 0],
                device_id={"tile": tile + 1},
                device_id_type=MESH,
            ).start()

    def halo(n, slot, c, side):
        landing = pl.ds(pl.multiple_of(PAD + c * rows, 8), rows)
        if side == 0:
            source, target, other = pl.ds(4, 4), pl.ds(4 + width, 4), tile - 1
        else:
            source, target, other = pl.ds(width, 4), pl.ds(0, 4), tile + 1
        return pltpu.make_async_remote_copy(
            field.at[slot, :, source, landing],
            field.at[slot, :, target, landing],
            halo_send.at[n, c, side],
            halo_recv.at[n, c, 1 - side],
            device_id={"tile": other},
            device_id_type=MESH,
        )

    for k in range(1, n_shot):
        pltpu.make_async_remote_copy(
            velocity,
            speed.at[:, owner_rows(shot, pair)],
            speed_send.at[k],
            speed_recv.at[k],
            device_id={"shot": lax.rem(shot + k, n_shot)},
            device_id_type=MESH,
        ).start()
    pltpu.make_async_remote_copy(
        velocity,
        speed.at[:, owner_rows(shot, pair)],
        mate_speed_send.at[0],
        mate_speed_recv.at[0],
        device_id={"pair": mate},
        device_id_type=MESH,
    ).start()
    for c in range(CHUNKS):
        start_halo(c, 0, source_now)
        start_halo(c, 1, recv_now)

    for slot in range(2):
        for f in range(2):
            field[slot, f, 4 : 4 + width, 0:PAD] = jnp.zeros((width, PAD, downward), jnp.float32)
            field[slot, f, 4 : 4 + width, PAD + across : 2 * PAD + across] = jnp.zeros((width, PAD, downward), jnp.float32)

    def clear(first):
        def body(i, _):
            field[i // 8, (i // 4) % 2, first + i % 4] = jnp.zeros((across + 2 * PAD, downward), jnp.float32)
            return 0

        lax.fori_loop(0, 16, body, 0)

    @pl.when(jnp.logical_not(has_low))
    def _():
        clear(0)

    @pl.when(jnp.logical_not(has_high))
    def _():
        clear(4 + width)

    def clear_image(i, _):
        stacked[i] = jnp.zeros((2 * margin + across, downward), jnp.float32)
        return 0

    lax.fori_loop(0, width, clear_image, 0)

    first = tile * width
    place = (recv_x[...] - first) * across + recv_yz[...] // downward
    depth = recv_yz[...] % downward
    receivers = record.shape[2]
    cell = lax.broadcasted_iota(jnp.int32, (width * across, receivers), 0)
    pick = jnp.where(cell == place, 1.0, 0.0).astype(jnp.bfloat16)
    at_depth = lax.broadcasted_iota(jnp.int32, (downward, receivers), 0) == depth

    def inject(n, _):
        amount = record[0, pl.ds(n, 1), :]
        high = amount.astype(jnp.bfloat16).astype(jnp.float32)
        rest = amount - high
        middle = rest.astype(jnp.bfloat16).astype(jnp.float32)
        low = rest - middle
        dense = jnp.zeros((width * across, downward), jnp.float32)
        for piece in (low, middle, high):
            spread = jnp.where(at_depth, piece, 0.0).astype(jnp.bfloat16)
            dense = dense + lax.dot_general(
                pick, spread, (((1,), (1,)), ((), ())), preferred_element_type=jnp.float32
            )
        injected[n] = dense.reshape(width, across, downward)
        return 0

    lax.fori_loop(0, STEPS, inject, 0)

    for k in range(1, n_shot):
        origin = lax.rem(shot + n_shot - k, n_shot)
        block = speed.at[:, owner_rows(origin, pair)]
        pltpu.make_async_remote_copy(
            velocity, block, speed_send.at[k], speed_recv.at[k], device_id={"pair": mate}, device_id_type=MESH
        ).wait()
        pltpu.make_async_remote_copy(
            block, block, mate_speed_send.at[k], mate_speed_recv.at[k], device_id={"pair": mate}, device_id_type=MESH
        ).start()
    for copy in loads:
        copy.wait()
    for k in range(n_shot):
        origin = lax.rem(shot + n_shot - k, n_shot)
        pltpu.make_async_remote_copy(
            velocity,
            speed.at[:, owner_rows(origin, mate)],
            mate_speed_send.at[k],
            mate_speed_recv.at[k],
            device_id={"pair": mate},
            device_id_type=MESH,
        ).wait()

    start_row = anchors[0]

    def refresh(i, _):
        scaled = speed[i, pl.ds(start_row, across), :] * courant_scale
        courant[i] = scaled * scaled
        return 0

    lax.fori_loop(0, width, refresh, 0)

    lane = lax.broadcasted_iota(jnp.int32, (1, 1, downward), 2)
    behind = [jnp.where(lane >= r, stencil_weights[r], 0.0) for r in range(1, 5)]
    ahead = [jnp.where(lane < downward - r, stencil_weights[r], 0.0) for r in range(1, 5)]
    shape = (width, 8, downward)
    local_cell = (
        lax.broadcasted_iota(jnp.int32, shape, 0) * (across * downward)
        + lax.broadcasted_iota(jnp.int32, shape, 1) * downward
        + lax.broadcasted_iota(jnp.int32, shape, 2)
    )
    source_cell = (source_x[0] - first) * (across * downward) + source_yz[0]

    def update(s, slot, y0):
        at = pl.multiple_of(PAD + y0, 8)
        gain = courant[:, pl.ds(y0, 8), :]
        results = []
        for f in range(2):
            column = field[slot, f, :, pl.ds(at, 8), :]
            centre = column[4 : 4 + width]
            sums = (3.0 * stencil_weights[0]) * centre
            for r in range(1, 5):
                near = column[4 - r : 4 - r + width] + column[4 + r : 4 + r + width]
                near = near + field[slot, f, 4 : 4 + width, pl.ds(at - r, 8), :]
                near = near + field[slot, f, 4 : 4 + width, pl.ds(at + r, 8), :]
                sums = sums + stencil_weights[r] * near
                sums = sums + behind[r - 1] * pltpu.roll(centre, r, 2)
                sums = sums + ahead[r - 1] * pltpu.roll(centre, downward - r, 2)
            older = field[1 - slot, f, 4 : 4 + width, pl.ds(at, 8), :]
            fresh = 2.0 * centre - older + gain * sums
            if f == 0:
                fresh = fresh + jnp.where(local_cell == source_cell - y0 * downward, wavelet[0, s], 0.0)
            else:
                fresh = fresh + injected[s, :, pl.ds(y0, 8), :]
            field[1 - slot, f, 4 : 4 + width, pl.ds(at, 8), :] = fresh
            results.append(fresh)
        spot = pl.ds(pl.multiple_of(margin + y0, 8), 8)
        stacked[:, spot, :] = stacked[:, spot, :] + results[0] * results[1]

    def step(s, _):
        slot = lax.rem(s, 2)

        def chunk(c, _):
            @pl.when(has_low)
            def _():
                halo(s, slot, c, 1).wait_recv()

            @pl.when(has_high)
            def _():
                halo(s, slot, c, 0).wait_recv()

            @pl.when(jnp.logical_and(has_low, s > 0))
            def _():
                halo(s - 1, 1 - slot, c, 0).wait_send()

            @pl.when(jnp.logical_and(has_high, s > 0))
            def _():
                halo(s - 1, 1 - slot, c, 1).wait_send()

            def tiles(t, _):
                update(s, slot, pl.multiple_of(c * rows + t * 8, 8))
                return 0

            lax.fori_loop(0, rows // 8, tiles, 0)

            @pl.when(jnp.logical_and(has_low, s < STEPS - 1))
            def _():
                halo(s + 1, 1 - slot, c, 0).start()

            @pl.when(jnp.logical_and(has_high, s < STEPS - 1))
            def _():
                halo(s + 1, 1 - slot, c, 1).start()

            return 0

        lax.fori_loop(0, CHUNKS, chunk, 0)
        return 0

    lax.fori_loop(0, STEPS, step, 0)

    final = STEPS % 2
    stores = [
        pltpu.make_async_copy(field.at[final, 0, 4 : 4 + width, inner], source_out.at[0], out_sem.at[0]),
        pltpu.make_async_copy(field.at[final, 1, 4 : 4 + width, inner], recv_out.at[0], out_sem.at[1]),
    ]
    for copy in stores:
        copy.start()

    def contribution(s, p):
        return stacked[:, pl.ds((s * n_pair + p) * owned + margin - start_row, owned), :]

    for k in range(n_shot):
        mate_out[k] = contribution(lax.rem(shot + k, n_shot), mate)
        pltpu.make_async_remote_copy(
            mate_out.at[k],
            mate_in.at[k],
            mate_sem.at[0, k],
            mate_sem.at[1, k],
            device_id={"pair": mate},
            device_id_type=MESH,
        ).start()

    def mate_copy(k):
        return pltpu.make_async_remote_copy(
            mate_out.at[k],
            mate_in.at[k],
            mate_sem.at[0, k],
            mate_sem.at[1, k],
            device_id={"pair": mate},
            device_id_type=MESH,
        )

    def shot_copy(k):
        return pltpu.make_async_remote_copy(
            shot_out.at[k - 1],
            shot_in.at[k - 1],
            shot_send.at[k - 1],
            shot_recv.at[k - 1],
            device_id={"shot": lax.rem(shot + k, n_shot)},
            device_id_type=MESH,
        )

    for k in range(1, n_shot):
        mate_copy(k).wait_recv()
        shot_out[k - 1] = contribution(lax.rem(shot + k, n_shot), pair) + mate_in[k]
        shot_copy(k).start()
    mate_copy(0).wait_recv()
    mine = contribution(shot, pair) + mate_in[0]
    for k in range(1, n_shot):
        shot_copy(k).wait_recv()
        mine = mine + shot_in[k - 1]
    total[...] = mine
    last = pltpu.make_async_copy(total, image_out, out_sem.at[2])
    last.start()

    for c in range(CHUNKS):
        @pl.when(has_low)
        def _():
            halo(STEPS - 1, (STEPS - 1) % 2, c, 0).wait_send()

        @pl.when(has_high)
        def _():
            halo(STEPS - 1, (STEPS - 1) % 2, c, 1).wait_send()

    for k in range(n_shot):
        mate_copy(k).wait_send()
    for k in range(1, n_shot):
        shot_copy(k).wait_send()
    for copy in stores:
        copy.wait()
    last.wait()


def deliver(*refs):
    sem = refs[-1]
    count = (len(refs) - 1) // 2
    copies = [pltpu.make_async_copy(refs[i], refs[count + i], sem.at[i]) for i in range(count)]
    for copy in copies:
        copy.start()
    for copy in copies:
        copy.wait()


def solution(mesh):
    sizes = (mesh.shape["tile"], mesh.shape["shot"], mesh.shape["pair"])
    n_shot, n_pair = sizes[1:]

    def shards(velocity, anchors, source_prev, source_now, recv_prev, recv_now, source_x, source_yz, wavelet, recv_x, recv_yz, record):
        width, across, downward = source_now.shape[1:]
        owned = velocity.shape[1]
        survey = owned * n_shot * n_pair
        margin = survey - across
        f32 = jnp.float32
        block = (width, owned, downward)
        smem = pl.BlockSpec(memory_space=pltpu.SMEM)
        vmem = pl.BlockSpec(memory_space=pltpu.VMEM)
        anywhere = pl.BlockSpec(memory_space=pl.ANY)
        dma = pltpu.SemaphoreType.DMA
        results = pl.pallas_call(
            functools.partial(kernel, sizes),
            out_shape=(
                jax.ShapeDtypeStruct(velocity.shape, f32),
                jax.ShapeDtypeStruct(source_now.shape, f32),
                jax.ShapeDtypeStruct(recv_now.shape, f32),
            ),
            in_specs=[smem] * 4 + [vmem] * 3 + [anywhere] * 5,
            out_specs=(vmem,)*3,
            scratch_shapes=[
                pltpu.VMEM((2, 2, width + 8, across + 2 * PAD, downward), f32),
                pltpu.VMEM((width, survey, downward), f32),
                pltpu.VMEM((width, across, downward), f32),
                pltpu.VMEM((STEPS, width, across, downward), f32),
                pltpu.VMEM((width, across + 2 * margin, downward), f32),
                pltpu.VMEM((n_shot,) + block, f32),
                pltpu.VMEM((n_shot,) + block, f32),
                pltpu.VMEM((n_shot - 1,) + block, f32),
                pltpu.VMEM((n_shot - 1,) + block, f32),
                pltpu.VMEM(block, f32),
                dma((5,)),
                dma((STEPS, CHUNKS, 2)),
                dma((STEPS, CHUNKS, 2)),
                dma((n_shot,)),
                dma((n_shot,)),
                dma((n_shot,)),
                dma((n_shot,)),
                dma((2, n_shot)),
                dma((n_shot - 1,)),
                dma((n_shot - 1,)),
                dma((3,)),
            ],
            compiler_params=pltpu.CompilerParams(
                collective_id=0, has_side_effects=True, vmem_limit_bytes=63 * 1024 * 1024
            ),
        )(anchors, source_x, source_yz, wavelet, recv_x, recv_yz, record, velocity, source_prev, source_now, recv_prev, recv_now)

        return pl.pallas_call(
            deliver,
            out_shape=[jax.ShapeDtypeStruct(result.shape, f32) for result in results],
            in_specs=[vmem]*3,
            out_specs=[anywhere] * 3,
            scratch_shapes=[dma((3,))],
        )(*results)

    in_specs = (
        P(("region", "tile"), ("shot", "pair"), None),
        P(("region", "shot")),
        P(("region", "shot", "pair"), "tile", None, None),
        P(("region", "shot", "pair"), "tile", None, None),
        P(("region", "shot", "pair"), "tile", None, None),
        P(("region", "shot", "pair"), "tile", None, None),
        P(("region", "shot", "pair")),
        P(("region", "shot", "pair")),
        P(("region", "shot", "pair"), None),
        P(("region", "shot", "pair"), None),
        P(("region", "shot", "pair"), None),
        P(("region", "shot", "pair"), None, None),
    )
    out_specs = (
        P(("region", "tile"), ("shot", "pair"), None),
        P(("region", "shot", "pair"), "tile", None, None),
        P(("region", "shot", "pair"), "tile", None, None),
    )
    return jax.shard_map(shards, mesh=mesh, in_specs=in_specs, out_specs=out_specs, check_vma=False)
```

```python
import functools

import jax
import jax.numpy as jnp
from jax import lax
from jax.experimental import pallas as pl
from jax.experimental.pallas import tpu as pltpu
from jax.sharding import PartitionSpec as P

STEPS = 6
MESH = pl.DeviceIdType.MESH

stencil_weights = (-205.0 / 72.0, 8.0 / 5.0, -1.0 / 5.0, 8.0 / 315.0, -1.0 / 560.0)
courant_scale = 0.1

PAD = 8
CHUNKS = 2


def kernel(
    sizes,
    anchors,
    source_x,
    source_yz,
    wavelet,
    recv_x,
    recv_yz,
    record,
    velocity,
    source_prev,
    source_now,
    recv_prev,
    recv_now,
    image_out,
    source_out,
    recv_out,
    field,
    speed,
    courant,
    injected,
    pending,
    stacked,
    mate_out,
    mate_in,
    shot_out,
    shot_in,
    load_sem,
    halo_send,
    halo_recv,
    speed_send,
    speed_recv,
    mate_speed_send,
    mate_speed_recv,
    mate_sem,
    shot_send,
    shot_recv,
    out_sem,
):
    n_tile, n_shot, n_pair = sizes
    width, across, downward = source_now.shape[1:]
    owned = velocity.shape[1]
    survey = owned * n_shot * n_pair
    margin = survey - across
    rows = across // CHUNKS
    tile = lax.axis_index("tile")
    shot = lax.axis_index("shot")
    pair = lax.axis_index("pair")
    mate = 1 - pair
    has_low = tile > 0
    has_high = tile < n_tile - 1

    barrier = pltpu.get_barrier_semaphore()

    @pl.when(has_low)
    def _():
        pl.semaphore_signal(barrier, inc=1, device_id={"tile": tile - 1}, device_id_type=MESH)

    @pl.when(has_high)
    def _():
        pl.semaphore_signal(barrier, inc=1, device_id={"tile": tile + 1}, device_id_type=MESH)

    pl.semaphore_signal(barrier, inc=1, device_id={"pair": mate}, device_id_type=MESH)
    for k in range(1, n_shot):
        pl.semaphore_signal(barrier, inc=1, device_id={"shot": lax.rem(shot + k, n_shot)}, device_id_type=MESH)

    def owner_rows(s, p):
        return pl.ds(pl.multiple_of((s * n_pair + p) * owned, owned), owned)

    inner = pl.ds(PAD, across)
    loads = [
        pltpu.make_async_copy(source_now.at[0], field.at[0, 0, 4 : 4 + width, inner], load_sem.at[0]),
        pltpu.make_async_copy(recv_now.at[0], field.at[0, 1, 4 : 4 + width, inner], load_sem.at[1]),
        pltpu.make_async_copy(source_prev.at[0], field.at[1, 0, 4 : 4 + width, inner], load_sem.at[2]),
        pltpu.make_async_copy(recv_prev.at[0], field.at[1, 1, 4 : 4 + width, inner], load_sem.at[3]),
        pltpu.make_async_copy(velocity, speed.at[:, owner_rows(shot, pair)], load_sem.at[4]),
    ]
    for copy in loads:
        copy.start()

    neighbours = n_shot + has_low.astype(jnp.int32) + has_high.astype(jnp.int32)
    pl.semaphore_wait(barrier, neighbours)

    def start_halo(c, f, now):
        part = pl.ds(pl.multiple_of(c * rows, rows), rows)
        landing = pl.ds(pl.multiple_of(PAD + c * rows, 8), rows)

        @pl.when(has_low)
        def _():
            pltpu.make_async_remote_copy(
                now.at[0, 0:4, part],
                field.at[0, f, 4 + width : 8 + width, landing],
                halo_send.at[0, c, 0],
                halo_recv.at[0, c, 1],
                device_id={"tile": tile - 1},
                device_id_type=MESH,
            ).start()

        @pl.when(has_high)
        def _():
            pltpu.make_async_remote_copy(
                now.at[0, width - 4 : width, part],
                field.at[0, f, 0:4, landing],
                halo_send.at[0, c, 1],
                halo_recv.at[0, c, 0],
                device_id={"tile": tile + 1},
                device_id_type=MESH,
            ).start()

    def halo(n, slot, c, side):
        landing = pl.ds(pl.multiple_of(PAD + c * rows, 8), rows)
        if side == 0:
            source, target, other = pl.ds(4, 4), pl.ds(4 + width, 4), tile - 1
        else:
            source, target, other = pl.ds(width, 4), pl.ds(0, 4), tile + 1
        return pltpu.make_async_remote_copy(
            field.at[slot, :, source, landing],
            field.at[slot, :, target, landing],
            halo_send.at[n, c, side],
            halo_recv.at[n, c, 1 - side],
            device_id={"tile": other},
            device_id_type=MESH,
        )

    for k in range(1, n_shot):
        pltpu.make_async_remote_copy(
            velocity,
            speed.at[:, owner_rows(shot, pair)],
            speed_send.at[k],
            speed_recv.at[k],
            device_id={"shot": lax.rem(shot + k, n_shot)},
            device_id_type=MESH,
        ).start()
    pltpu.make_async_remote_copy(
        velocity,
        speed.at[:, owner_rows(shot, pair)],
        mate_speed_send.at[0],
        mate_speed_recv.at[0],
        device_id={"pair": mate},
        device_id_type=MESH,
    ).start()
    for c in range(CHUNKS):
        start_halo(c, 0, source_now)
        start_halo(c, 1, recv_now)

    for slot in range(2):
        for f in range(2):
            field[slot, f, 4 : 4 + width, 0:PAD] = jnp.zeros((width, PAD, downward), jnp.float32)
            field[slot, f, 4 : 4 + width, PAD + across : 2 * PAD + across] = jnp.zeros((width, PAD, downward), jnp.float32)

    def clear(first):
        def body(i, _):
            field[i // 8, (i // 4) % 2, first + i % 4] = jnp.zeros((across + 2 * PAD, downward), jnp.float32)
            return 0

        lax.fori_loop(0, 16, body, 0)

    @pl.when(jnp.logical_not(has_low))
    def _():
        clear(0)

    @pl.when(jnp.logical_not(has_high))
    def _():
        clear(4 + width)

    def clear_image(i, _):
        stacked[i] = jnp.zeros((2 * margin + across, downward), jnp.float32)
        return 0

    lax.fori_loop(0, width, clear_image, 0)

    first = tile * width
    place = (recv_x[...] - first) * across + recv_yz[...] // downward
    depth = recv_yz[...] % downward
    receivers = record.shape[2]
    cell = lax.broadcasted_iota(jnp.int32, (width * across, receivers), 0)
    pick = jnp.where(cell == place, 1.0, 0.0).astype(jnp.bfloat16)
    at_depth = lax.broadcasted_iota(jnp.int32, (downward, receivers), 0) == depth

    def inject(n):
        amount = record[n]
        high = amount.astype(jnp.bfloat16).astype(jnp.float32)
        rest = amount - high
        middle = rest.astype(jnp.bfloat16).astype(jnp.float32)
        low = rest - middle
        dense = jnp.zeros((width * across, downward), jnp.float32)
        for piece in (low, middle, high):
            spread = jnp.where(at_depth, piece, 0.0).astype(jnp.bfloat16)
            dense = dense + lax.dot_general(
                pick, spread, (((1,), (1,)), ((), ())), preferred_element_type=jnp.float32
            )
        injected[...] = dense.reshape(width, across, downward)

    lane = lax.broadcasted_iota(jnp.int32, (1, 1, downward), 2)
    behind = [jnp.where(lane >= r, stencil_weights[r], 0.0) for r in range(1, 5)]
    ahead = [jnp.where(lane < downward - r, stencil_weights[r], 0.0) for r in range(1, 5)]
    shape = (width, 8, downward)
    local_cell = (
        lax.broadcasted_iota(jnp.int32, shape, 0) * (across * downward)
        + lax.broadcasted_iota(jnp.int32, shape, 1) * downward
        + lax.broadcasted_iota(jnp.int32, shape, 2)
    )
    source_cell = (source_x[0] - first) * (across * downward) + source_yz[0]

    def prepare(s, slot, y0):
        at = pl.multiple_of(PAD + y0, 8)
        for f in range(2):
            centre = field[slot, f, 4 : 4 + width, pl.ds(at, 8), :]
            sums = (3.0 * stencil_weights[0]) * centre
            for r in range(1, 5):
                layers = []
                for j in range(width):
                    layer = [centre[i : i + 1] for i in (j - r, j + r) if 0 <= i < width]
                    layers.append(layer[0] if len(layer) == 1 else layer[0] + layer[1])
                near = jnp.concatenate(layers, axis=0)
                near = near + field[slot, f, 4 : 4 + width, pl.ds(at - r, 8), :]
                near = near + field[slot, f, 4 : 4 + width, pl.ds(at + r, 8), :]
                sums = sums + stencil_weights[r] * near
                sums = sums + behind[r - 1] * pltpu.roll(centre, r, 2)
                sums = sums + ahead[r - 1] * pltpu.roll(centre, downward - r, 2)
            older = field[1 - slot, f, 4 : 4 + width, pl.ds(at, 8), :]
            pending[f, :, pl.ds(y0, 8), :] = sums
            fresh = 2.0 * centre - older
            if f == 0:
                fresh = fresh + jnp.where(local_cell == source_cell - y0 * downward, wavelet[0, s], 0.0)
            else:
                fresh = fresh + injected[:, pl.ds(y0, 8), :]
            field[1 - slot, f, 4 : 4 + width, pl.ds(at, 8), :] = fresh

    def complete(slot, y0):
        at = pl.multiple_of(PAD + y0, 8)
        gain = courant[:, pl.ds(y0, 8), :]
        results = []
        for f in range(2):
            low = field[slot, f, 0:4, pl.ds(at, 8), :]
            high = field[slot, f, 4 + width : 8 + width, pl.ds(at, 8), :]
            below, above = [], []
            for j in range(4):
                term = stencil_weights[j + 1] * low[3:4]
                for r in range(j + 2, 5):
                    term = term + stencil_weights[r] * low[4 + j - r : 5 + j - r]
                below.append(term)
                term = stencil_weights[4 - j] * high[0:1]
                for r in range(5 - j, 5):
                    term = term + stencil_weights[r] * high[j - 4 + r : j - 3 + r]
                above.append(term)
            middle = [jnp.zeros((width - 8, 8, downward), jnp.float32)] if width > 8 else []
            outer = jnp.concatenate(below + middle + above, axis=0)
            fresh = field[1 - slot, f, 4 : 4 + width, pl.ds(at, 8), :] + gain * (pending[f, :, pl.ds(y0, 8), :] + outer)
            field[1 - slot, f, 4 : 4 + width, pl.ds(at, 8), :] = fresh
            results.append(fresh)
        spot = pl.ds(pl.multiple_of(margin + y0, 8), 8)
        stacked[:, spot, :] = stacked[:, spot, :] + results[0] * results[1]

    def settle(s, c, _):
        @pl.when(has_low)
        def _():
            halo(s, lax.rem(s, 2), c, 0).wait_send()

        @pl.when(has_high)
        def _():
            halo(s, lax.rem(s, 2), c, 1).wait_send()

        return 0

    def prepare_all(s):
        inject(s)

        def ready(t, _):
            prepare(s, lax.rem(s, 2), pl.multiple_of(t * 8, 8))
            return 0

        lax.fori_loop(0, across // 8, ready, 0)

    for copy in loads[:4]:
        copy.wait()
    prepare_all(0)

    for k in range(1, n_shot):
        origin = lax.rem(shot + n_shot - k, n_shot)
        block = speed.at[:, owner_rows(origin, pair)]
        pltpu.make_async_remote_copy(
            velocity, block, speed_send.at[k], speed_recv.at[k], device_id={"pair": mate}, device_id_type=MESH
        ).wait()
        pltpu.make_async_remote_copy(
            block, block, mate_speed_send.at[k], mate_speed_recv.at[k], device_id={"pair": mate}, device_id_type=MESH
        ).start()
    loads[4].wait()
    for k in range(n_shot):
        origin = lax.rem(shot + n_shot - k, n_shot)
        pltpu.make_async_remote_copy(
            velocity,
            speed.at[:, owner_rows(origin, mate)],
            mate_speed_send.at[k],
            mate_speed_recv.at[k],
            device_id={"pair": mate},
            device_id_type=MESH,
        ).wait()

    start_row = anchors[0]

    def refresh(i, _):
        scaled = speed[i, pl.ds(start_row, across), :] * courant_scale
        courant[i] = scaled * scaled
        return 0

    lax.fori_loop(0, width, refresh, 0)

    def step(s, _):
        slot = lax.rem(s, 2)

        def chunk(c, _):
            @pl.when(has_low)
            def _():
                halo(s, slot, c, 1).wait_recv()

            @pl.when(has_high)
            def _():
                halo(s, slot, c, 0).wait_recv()

            def tiles(t, _):
                complete(slot, pl.multiple_of(c * rows + t * 8, 8))
                return 0

            lax.fori_loop(0, rows // 8, tiles, 0)

            @pl.when(jnp.logical_and(has_low, s < STEPS - 1))
            def _():
                halo(s + 1, 1 - slot, c, 0).start()

            @pl.when(jnp.logical_and(has_high, s < STEPS - 1))
            def _():
                halo(s + 1, 1 - slot, c, 1).start()

            return 0

        lax.fori_loop(0, CHUNKS, chunk, 0)

        @pl.when(s < STEPS - 1)
        def _():
            lax.fori_loop(0, CHUNKS, functools.partial(settle, s), 0)
            prepare_all(s + 1)

        return 0

    lax.fori_loop(0, STEPS, step, 0)

    final = STEPS % 2
    stores = [
        pltpu.make_async_copy(field.at[final, 0, 4 : 4 + width, inner], source_out.at[0], out_sem.at[0]),
        pltpu.make_async_copy(field.at[final, 1, 4 : 4 + width, inner], recv_out.at[0], out_sem.at[1]),
    ]
    for copy in stores:
        copy.start()

    def contribution(s, p):
        return stacked[:, pl.ds((s * n_pair + p) * owned + margin - start_row, owned), :]

    for k in range(n_shot):
        mate_out[k] = contribution(lax.rem(shot + k, n_shot), mate)
        pltpu.make_async_remote_copy(
            mate_out.at[k],
            mate_in.at[k],
            mate_sem.at[0, k],
            mate_sem.at[1, k],
            device_id={"pair": mate},
            device_id_type=MESH,
        ).start()

    def mate_copy(k):
        return pltpu.make_async_remote_copy(
            mate_out.at[k],
            mate_in.at[k],
            mate_sem.at[0, k],
            mate_sem.at[1, k],
            device_id={"pair": mate},
            device_id_type=MESH,
        )

    def shot_copy(k):
        return pltpu.make_async_remote_copy(
            shot_out.at[k - 1],
            shot_in.at[k - 1],
            shot_send.at[k - 1],
            shot_recv.at[k - 1],
            device_id={"shot": lax.rem(shot + k, n_shot)},
            device_id_type=MESH,
        )

    for k in range(1, n_shot):
        mate_copy(k).wait_recv()
        shot_out[k - 1] = contribution(lax.rem(shot + k, n_shot), pair) + mate_in[k]
        shot_copy(k).start()
    mate_copy(0).wait_recv()
    mine = contribution(shot, pair) + mate_in[0]
    for k in range(1, n_shot):
        shot_copy(k).wait_recv()
        mine = mine + shot_in[k - 1]
    image_out[...] = mine

    for c in range(CHUNKS):
        @pl.when(has_low)
        def _():
            halo(STEPS - 1, (STEPS - 1) % 2, c, 0).wait_send()

        @pl.when(has_high)
        def _():
            halo(STEPS - 1, (STEPS - 1) % 2, c, 1).wait_send()

    for k in range(n_shot):
        mate_copy(k).wait_send()
    for k in range(1, n_shot):
        shot_copy(k).wait_send()
    for copy in stores:
        copy.wait()


def deliver(*refs):
    sem = refs[-1]
    count = (len(refs) - 1) // 2
    copies = [pltpu.make_async_copy(refs[i], refs[count + i], sem.at[i]) for i in range(count)]
    for copy in copies:
        copy.start()
    for copy in copies:
        copy.wait()


def solution(mesh):
    sizes = (mesh.shape["tile"], mesh.shape["shot"], mesh.shape["pair"])
    n_shot, n_pair = sizes[1:]

    def shards(velocity, anchors, source_prev, source_now, recv_prev, recv_now, source_x, source_yz, wavelet, recv_x, recv_yz, record):
        width, across, downward = source_now.shape[1:]
        owned = velocity.shape[1]
        survey = owned * n_shot * n_pair
        margin = survey - across
        f32 = jnp.float32
        block = (width, owned, downward)
        smem = pl.BlockSpec(memory_space=pltpu.SMEM)
        vmem = pl.BlockSpec(memory_space=pltpu.VMEM)
        anywhere = pl.BlockSpec(memory_space=pl.ANY)
        dma = pltpu.SemaphoreType.DMA
        results = pl.pallas_call(
            functools.partial(kernel, sizes),
            out_shape=(
                jax.ShapeDtypeStruct(velocity.shape, f32),
                jax.ShapeDtypeStruct(source_now.shape, f32),
                jax.ShapeDtypeStruct(recv_now.shape, f32),
            ),
            in_specs=[smem] * 4 + [vmem] * 3 + [anywhere] * 5,
            out_specs=(vmem,)*3,
            scratch_shapes=[
                pltpu.VMEM((2, 2, width + 8, across + 2 * PAD, downward), f32),
                pltpu.VMEM((width, survey, downward), f32),
                pltpu.VMEM((width, across, downward), f32),
                pltpu.VMEM((width, across, downward), f32),
                pltpu.VMEM((2, width, across, downward), f32),
                pltpu.VMEM((width, across + 2 * margin, downward), f32),
                pltpu.VMEM((n_shot,) + block, f32),
                pltpu.VMEM((n_shot,) + block, f32),
                pltpu.VMEM((n_shot - 1,) + block, f32),
                pltpu.VMEM((n_shot - 1,) + block, f32),
                dma((5,)),
                dma((STEPS, CHUNKS, 2)),
                dma((STEPS, CHUNKS, 2)),
                dma((n_shot,)),
                dma((n_shot,)),
                dma((n_shot,)),
                dma((n_shot,)),
                dma((2, n_shot)),
                dma((n_shot - 1,)),
                dma((n_shot - 1,)),
                dma((2,)),
            ],
            compiler_params=pltpu.CompilerParams(
                collective_id=0, has_side_effects=True, vmem_limit_bytes=63 * 1024 * 1024
            ),
        )(anchors, source_x, source_yz, wavelet, recv_x, recv_yz, jnp.swapaxes(record, 0, 1), velocity, source_prev, source_now, recv_prev, recv_now)

        return pl.pallas_call(
            deliver,
            out_shape=[jax.ShapeDtypeStruct(result.shape, f32) for result in results],
            in_specs=[vmem]*3,
            out_specs=[anywhere] * 3,
            scratch_shapes=[dma((3,))],
        )(*results)

    in_specs = (
        P(("region", "tile"), ("shot", "pair"), None),
        P(("region", "shot")),
        P(("region", "shot", "pair"), "tile", None, None),
        P(("region", "shot", "pair"), "tile", None, None),
        P(("region", "shot", "pair"), "tile", None, None),
        P(("region", "shot", "pair"), "tile", None, None),
        P(("region", "shot", "pair")),
        P(("region", "shot", "pair")),
        P(("region", "shot", "pair"), None),
        P(("region", "shot", "pair"), None),
        P(("region", "shot", "pair"), None),
        P(("region", "shot", "pair"), None, None),
    )
    out_specs = (
        P(("region", "tile"), ("shot", "pair"), None),
        P(("region", "shot", "pair"), "tile", None, None),
        P(("region", "shot", "pair"), "tile", None, None),
    )
    return jax.shard_map(shards, mesh=mesh, in_specs=in_specs, out_specs=out_specs, check_vma=False)
```

```python
import functools

import jax
import jax.numpy as jnp
from jax import lax
from jax.experimental import pallas as pl
from jax.experimental.pallas import tpu as pltpu
from jax.sharding import PartitionSpec as P

STEPS = 6
MESH = pl.DeviceIdType.MESH

stencil_weights = (-205.0 / 72.0, 8.0 / 5.0, -1.0 / 5.0, 8.0 / 315.0, -1.0 / 560.0)
courant_scale = 0.1

PAD = 8
CHUNKS = 2
PIECES = 2


def kernel(
    sizes,
    anchors,
    source_x,
    source_yz,
    wavelet,
    recv_x,
    recv_yz,
    record,
    velocity,
    source_prev,
    source_now,
    recv_prev,
    recv_now,
    image_out,
    source_out,
    recv_out,
    field,
    speed,
    courant,
    injected,
    pending,
    stacked,
    mate_out,
    mate_in,
    shot_out,
    shot_in,
    load_sem,
    halo_send,
    halo_recv,
    speed_send,
    speed_recv,
    mate_speed_send,
    mate_speed_recv,
    mate_sem,
    shot_send,
    shot_recv,
    out_sem,
):
    n_tile, n_shot, n_pair = sizes
    width, across, downward = source_now.shape[1:]
    owned = velocity.shape[1]
    survey = owned * n_shot * n_pair
    margin = survey - across
    rows = across // CHUNKS
    tile = lax.axis_index("tile")
    shot = lax.axis_index("shot")
    pair = lax.axis_index("pair")
    mate = 1 - pair
    has_low = tile > 0
    has_high = tile < n_tile - 1

    barrier = pltpu.get_barrier_semaphore()

    @pl.when(has_low)
    def _():
        pl.semaphore_signal(barrier, inc=1, device_id={"tile": tile - 1}, device_id_type=MESH)

    @pl.when(has_high)
    def _():
        pl.semaphore_signal(barrier, inc=1, device_id={"tile": tile + 1}, device_id_type=MESH)

    pl.semaphore_signal(barrier, inc=1, device_id={"pair": mate}, device_id_type=MESH)
    for k in range(1, n_shot):
        pl.semaphore_signal(barrier, inc=1, device_id={"shot": lax.rem(shot + k, n_shot)}, device_id_type=MESH)

    def owner_rows(s, p):
        return pl.ds(pl.multiple_of((s * n_pair + p) * owned, owned), owned)

    inner = pl.ds(PAD, across)
    loads = [
        pltpu.make_async_copy(source_now.at[0], field.at[0, 0, 4 : 4 + width, inner], load_sem.at[0]),
        pltpu.make_async_copy(recv_now.at[0], field.at[0, 1, 4 : 4 + width, inner], load_sem.at[1]),
        pltpu.make_async_copy(source_prev.at[0], field.at[1, 0, 4 : 4 + width, inner], load_sem.at[2]),
        pltpu.make_async_copy(recv_prev.at[0], field.at[1, 1, 4 : 4 + width, inner], load_sem.at[3]),
        pltpu.make_async_copy(velocity, speed.at[:, owner_rows(shot, pair)], load_sem.at[4]),
    ]
    for copy in loads:
        copy.start()

    neighbours = n_shot + has_low.astype(jnp.int32) + has_high.astype(jnp.int32)
    pl.semaphore_wait(barrier, neighbours)

    def start_halo(c, f, now):
        part = pl.ds(pl.multiple_of(c * rows, rows), rows)
        landing = pl.ds(pl.multiple_of(PAD + c * rows, 8), rows)

        @pl.when(has_low)
        def _():
            pltpu.make_async_remote_copy(
                now.at[0, 0:4, part],
                field.at[0, f, 4 + width : 8 + width, landing],
                halo_send.at[0, c, 0],
                halo_recv.at[0, c, 1],
                device_id={"tile": tile - 1},
                device_id_type=MESH,
            ).start()

        @pl.when(has_high)
        def _():
            pltpu.make_async_remote_copy(
                now.at[0, width - 4 : width, part],
                field.at[0, f, 0:4, landing],
                halo_send.at[0, c, 1],
                halo_recv.at[0, c, 0],
                device_id={"tile": tile + 1},
                device_id_type=MESH,
            ).start()

    def halo(n, slot, c, side):
        landing = pl.ds(pl.multiple_of(PAD + c * rows, 8), rows)
        if side == 0:
            source, target, other = pl.ds(4, 4), pl.ds(4 + width, 4), tile - 1
        else:
            source, target, other = pl.ds(width, 4), pl.ds(0, 4), tile + 1
        return pltpu.make_async_remote_copy(
            field.at[slot, :, source, landing],
            field.at[slot, :, target, landing],
            halo_send.at[n, c, side],
            halo_recv.at[n, c, 1 - side],
            device_id={"tile": other},
            device_id_type=MESH,
        )

    for k in range(1, n_shot):
        pltpu.make_async_remote_copy(
            velocity,
            speed.at[:, owner_rows(shot, pair)],
            speed_send.at[k],
            speed_recv.at[k],
            device_id={"shot": lax.rem(shot + k, n_shot)},
            device_id_type=MESH,
        ).start()
    pltpu.make_async_remote_copy(
        velocity,
        speed.at[:, owner_rows(shot, pair)],
        mate_speed_send.at[0],
        mate_speed_recv.at[0],
        device_id={"pair": mate},
        device_id_type=MESH,
    ).start()
    for c in range(CHUNKS):
        start_halo(c, 0, source_now)
        start_halo(c, 1, recv_now)

    for slot in range(2):
        for f in range(2):
            field[slot, f, 4 : 4 + width, 0:PAD] = jnp.zeros((width, PAD, downward), jnp.float32)
            field[slot, f, 4 : 4 + width, PAD + across : 2 * PAD + across] = jnp.zeros((width, PAD, downward), jnp.float32)

    def clear(first):
        def body(i, _):
            field[i // 8, (i // 4) % 2, first + i % 4] = jnp.zeros((across + 2 * PAD, downward), jnp.float32)
            return 0

        lax.fori_loop(0, 16, body, 0)

    @pl.when(jnp.logical_not(has_low))
    def _():
        clear(0)

    @pl.when(jnp.logical_not(has_high))
    def _():
        clear(4 + width)

    def clear_image(i, _):
        stacked[i] = jnp.zeros((2 * margin + across, downward), jnp.float32)
        return 0

    lax.fori_loop(0, width, clear_image, 0)

    first = tile * width
    place = (recv_x[...] - first) * across + recv_yz[...] // downward
    depth = recv_yz[...] % downward
    receivers = record.shape[2]
    cell = lax.broadcasted_iota(jnp.int32, (width * across, receivers), 0)
    pick = jnp.where(cell == place, 1.0, 0.0).astype(jnp.bfloat16)
    at_depth = lax.broadcasted_iota(jnp.int32, (downward, receivers), 0) == depth

    def inject(n):
        amount = record[n]
        high = amount.astype(jnp.bfloat16).astype(jnp.float32)
        rest = amount - high
        middle = rest.astype(jnp.bfloat16).astype(jnp.float32)
        low = rest - middle
        dense = jnp.zeros((width * across, downward), jnp.float32)
        for piece in (low, middle, high):
            spread = jnp.where(at_depth, piece, 0.0).astype(jnp.bfloat16)
            dense = dense + lax.dot_general(
                pick, spread, (((1,), (1,)), ((), ())), preferred_element_type=jnp.float32
            )
        injected[...] = dense.reshape(width, across, downward)

    lane = lax.broadcasted_iota(jnp.int32, (1, 1, downward), 2)
    behind = [jnp.where(lane >= r, stencil_weights[r], 0.0) for r in range(1, 5)]
    ahead = [jnp.where(lane < downward - r, stencil_weights[r], 0.0) for r in range(1, 5)]
    shape = (width, 8, downward)
    local_cell = (
        lax.broadcasted_iota(jnp.int32, shape, 0) * (across * downward)
        + lax.broadcasted_iota(jnp.int32, shape, 1) * downward
        + lax.broadcasted_iota(jnp.int32, shape, 2)
    )
    source_cell = (source_x[0] - first) * (across * downward) + source_yz[0]

    def prepare(s, slot, y0):
        at = pl.multiple_of(PAD + y0, 8)
        for f in range(2):
            centre = field[slot, f, 4 : 4 + width, pl.ds(at, 8), :]
            sums = (3.0 * stencil_weights[0]) * centre
            for r in range(1, 5):
                layers = []
                for j in range(width):
                    layer = [centre[i : i + 1] for i in (j - r, j + r) if 0 <= i < width]
                    layers.append(layer[0] if len(layer) == 1 else layer[0] + layer[1])
                near = jnp.concatenate(layers, axis=0)
                near = near + field[slot, f, 4 : 4 + width, pl.ds(at - r, 8), :]
                near = near + field[slot, f, 4 : 4 + width, pl.ds(at + r, 8), :]
                sums = sums + stencil_weights[r] * near
                sums = sums + behind[r - 1] * pltpu.roll(centre, r, 2)
                sums = sums + ahead[r - 1] * pltpu.roll(centre, downward - r, 2)
            older = field[1 - slot, f, 4 : 4 + width, pl.ds(at, 8), :]
            pending[f, :, pl.ds(y0, 8), :] = sums
            fresh = 2.0 * centre - older
            if f == 0:
                fresh = fresh + jnp.where(local_cell == source_cell - y0 * downward, wavelet[0, s], 0.0)
            else:
                fresh = fresh + injected[:, pl.ds(y0, 8), :]
            field[1 - slot, f, 4 : 4 + width, pl.ds(at, 8), :] = fresh

    def complete(slot, y0):
        at = pl.multiple_of(PAD + y0, 8)
        gain = courant[:, pl.ds(y0, 8), :]
        results = []
        for f in range(2):
            low = field[slot, f, 0:4, pl.ds(at, 8), :]
            high = field[slot, f, 4 + width : 8 + width, pl.ds(at, 8), :]
            below, above = [], []
            for j in range(4):
                term = stencil_weights[j + 1] * low[3:4]
                for r in range(j + 2, 5):
                    term = term + stencil_weights[r] * low[4 + j - r : 5 + j - r]
                below.append(term)
                term = stencil_weights[4 - j] * high[0:1]
                for r in range(5 - j, 5):
                    term = term + stencil_weights[r] * high[j - 4 + r : j - 3 + r]
                above.append(term)
            middle = [jnp.zeros((width - 8, 8, downward), jnp.float32)] if width > 8 else []
            outer = jnp.concatenate(below + middle + above, axis=0)
            fresh = field[1 - slot, f, 4 : 4 + width, pl.ds(at, 8), :] + gain * (pending[f, :, pl.ds(y0, 8), :] + outer)
            field[1 - slot, f, 4 : 4 + width, pl.ds(at, 8), :] = fresh
            results.append(fresh)
        spot = pl.ds(pl.multiple_of(margin + y0, 8), 8)
        stacked[:, spot, :] = stacked[:, spot, :] + results[0] * results[1]

    def settle(s, c, _):
        @pl.when(has_low)
        def _():
            halo(s, lax.rem(s, 2), c, 0).wait_send()

        @pl.when(has_high)
        def _():
            halo(s, lax.rem(s, 2), c, 1).wait_send()

        return 0

    def prepare_all(s):
        inject(s)

        def ready(t, _):
            prepare(s, lax.rem(s, 2), pl.multiple_of(t * 8, 8))
            return 0

        lax.fori_loop(0, across // 8, ready, 0)

    for copy in loads[:4]:
        copy.wait()
    prepare_all(0)

    for k in range(1, n_shot):
        origin = lax.rem(shot + n_shot - k, n_shot)
        block = speed.at[:, owner_rows(origin, pair)]
        pltpu.make_async_remote_copy(
            velocity, block, speed_send.at[k], speed_recv.at[k], device_id={"pair": mate}, device_id_type=MESH
        ).wait()
        pltpu.make_async_remote_copy(
            block, block, mate_speed_send.at[k], mate_speed_recv.at[k], device_id={"pair": mate}, device_id_type=MESH
        ).start()
    loads[4].wait()
    for k in range(n_shot):
        origin = lax.rem(shot + n_shot - k, n_shot)
        pltpu.make_async_remote_copy(
            velocity,
            speed.at[:, owner_rows(origin, mate)],
            mate_speed_send.at[k],
            mate_speed_recv.at[k],
            device_id={"pair": mate},
            device_id_type=MESH,
        ).wait()

    start_row = anchors[0]

    def refresh(i, _):
        scaled = speed[i, pl.ds(start_row, across), :] * courant_scale
        courant[i] = scaled * scaled
        return 0

    lax.fori_loop(0, width, refresh, 0)

    def step(s, _):
        slot = lax.rem(s, 2)

        def chunk(c, _):
            @pl.when(has_low)
            def _():
                halo(s, slot, c, 1).wait_recv()

            @pl.when(has_high)
            def _():
                halo(s, slot, c, 0).wait_recv()

            def tiles(t, _):
                complete(slot, pl.multiple_of(c * rows + t * 8, 8))
                return 0

            lax.fori_loop(0, rows // 8, tiles, 0)

            @pl.when(jnp.logical_and(has_low, s < STEPS - 1))
            def _():
                halo(s + 1, 1 - slot, c, 0).start()

            @pl.when(jnp.logical_and(has_high, s < STEPS - 1))
            def _():
                halo(s + 1, 1 - slot, c, 1).start()

            return 0

        lax.fori_loop(0, CHUNKS, chunk, 0)

        @pl.when(s < STEPS - 1)
        def _():
            lax.fori_loop(0, CHUNKS, functools.partial(settle, s), 0)
            prepare_all(s + 1)

        return 0

    lax.fori_loop(0, STEPS, step, 0)

    final = STEPS % 2
    stores = [
        pltpu.make_async_copy(field.at[final, 0, 4 : 4 + width, inner], source_out.at[0], out_sem.at[0]),
        pltpu.make_async_copy(field.at[final, 1, 4 : 4 + width, inner], recv_out.at[0], out_sem.at[1]),
    ]
    for copy in stores:
        copy.start()

    depth_of = width // PIECES
    pieces = [pl.ds(i * depth_of, depth_of) for i in range(PIECES)]

    def contribution(s, p, layers):
        return stacked[layers, pl.ds((s * n_pair + p) * owned + margin - start_row, owned), :]

    def mate_copy(k, i):
        return pltpu.make_async_remote_copy(
            mate_out.at[k, pieces[i]],
            mate_in.at[k, pieces[i]],
            mate_sem.at[0, k, i],
            mate_sem.at[1, k, i],
            device_id={"pair": mate},
            device_id_type=MESH,
        )

    def shot_copy(k, i):
        return pltpu.make_async_remote_copy(
            shot_out.at[k - 1, pieces[i]],
            shot_in.at[k - 1, pieces[i]],
            shot_send.at[k - 1, i],
            shot_recv.at[k - 1, i],
            device_id={"shot": lax.rem(shot + k, n_shot)},
            device_id_type=MESH,
        )

    order = [(k, i) for k in list(range(1, n_shot)) + [0] for i in range(PIECES)]
    travelling = order[: (n_shot - 1) * PIECES]
    for k, i in order:
        mate_out[k, pieces[i]] = contribution(lax.rem(shot + k, n_shot), mate, pieces[i])
        mate_copy(k, i).start()
    for k, i in travelling:
        mate_copy(k, i).wait_recv()
        shot_out[k - 1, pieces[i]] = contribution(lax.rem(shot + k, n_shot), pair, pieces[i]) + mate_in[k, pieces[i]]
        shot_copy(k, i).start()
    for i in range(PIECES):
        mate_copy(0, i).wait_recv()
        image_out[pieces[i]] = contribution(shot, pair, pieces[i]) + mate_in[0, pieces[i]]
    for k, i in travelling:
        shot_copy(k, i).wait_recv()
        image_out[pieces[i]] = image_out[pieces[i]] + shot_in[k - 1, pieces[i]]

    for c in range(CHUNKS):
        @pl.when(has_low)
        def _():
            halo(STEPS - 1, (STEPS - 1) % 2, c, 0).wait_send()

        @pl.when(has_high)
        def _():
            halo(STEPS - 1, (STEPS - 1) % 2, c, 1).wait_send()

    for k, i in order:
        mate_copy(k, i).wait_send()
    for k, i in travelling:
        shot_copy(k, i).wait_send()
    for copy in stores:
        copy.wait()


def deliver(*refs):
    sem = refs[-1]
    count = (len(refs) - 1) // 2
    copies = [pltpu.make_async_copy(refs[i], refs[count + i], sem.at[i]) for i in range(count)]
    for copy in copies:
        copy.start()
    for copy in copies:
        copy.wait()


def solution(mesh):
    sizes = (mesh.shape["tile"], mesh.shape["shot"], mesh.shape["pair"])
    n_shot, n_pair = sizes[1:]

    def shards(velocity, anchors, source_prev, source_now, recv_prev, recv_now, source_x, source_yz, wavelet, recv_x, recv_yz, record):
        width, across, downward = source_now.shape[1:]
        owned = velocity.shape[1]
        survey = owned * n_shot * n_pair
        margin = survey - across
        f32 = jnp.float32
        block = (width, owned, downward)
        smem = pl.BlockSpec(memory_space=pltpu.SMEM)
        vmem = pl.BlockSpec(memory_space=pltpu.VMEM)
        anywhere = pl.BlockSpec(memory_space=pl.ANY)
        dma = pltpu.SemaphoreType.DMA
        results = pl.pallas_call(
            functools.partial(kernel, sizes),
            out_shape=(
                jax.ShapeDtypeStruct(velocity.shape, f32),
                jax.ShapeDtypeStruct(source_now.shape, f32),
                jax.ShapeDtypeStruct(recv_now.shape, f32),
            ),
            in_specs=[smem] * 4 + [vmem] * 3 + [anywhere] * 5,
            out_specs=(vmem, anywhere, anywhere),
            scratch_shapes=[
                pltpu.VMEM((2, 2, width + 8, across + 2 * PAD, downward), f32),
                pltpu.VMEM((width, survey, downward), f32),
                pltpu.VMEM((width, across, downward), f32),
                pltpu.VMEM((width, across, downward), f32),
                pltpu.VMEM((2, width, across, downward), f32),
                pltpu.VMEM((width, across + 2 * margin, downward), f32),
                pltpu.VMEM((n_shot,) + block, f32),
                pltpu.VMEM((n_shot,) + block, f32),
                pltpu.VMEM((n_shot - 1,) + block, f32),
                pltpu.VMEM((n_shot - 1,) + block, f32),
                dma((5,)),
                dma((STEPS, CHUNKS, 2)),
                dma((STEPS, CHUNKS, 2)),
                dma((n_shot,)),
                dma((n_shot,)),
                dma((n_shot,)),
                dma((n_shot,)),
                dma((2, n_shot, PIECES)),
                dma((n_shot - 1, PIECES)),
                dma((n_shot - 1, PIECES)),
                dma((2,)),
            ],
            compiler_params=pltpu.CompilerParams(
                collective_id=0, has_side_effects=True, vmem_limit_bytes=63 * 1024 * 1024
            ),
        )(anchors, source_x, source_yz, wavelet, recv_x, recv_yz, jnp.swapaxes(record, 0, 1), velocity, source_prev, source_now, recv_prev, recv_now)

        return pl.pallas_call(
            deliver,
            out_shape=[jax.ShapeDtypeStruct(result.shape, f32) for result in results],
            in_specs=[vmem]*3,
            out_specs=[anywhere] * 3,
            scratch_shapes=[dma((3,))],
        )(*results)

    in_specs = (
        P(("region", "tile"), ("shot", "pair"), None),
        P(("region", "shot")),
        P(("region", "shot", "pair"), "tile", None, None),
        P(("region", "shot", "pair"), "tile", None, None),
        P(("region", "shot", "pair"), "tile", None, None),
        P(("region", "shot", "pair"), "tile", None, None),
        P(("region", "shot", "pair")),
        P(("region", "shot", "pair")),
        P(("region", "shot", "pair"), None),
        P(("region", "shot", "pair"), None),
        P(("region", "shot", "pair"), None),
        P(("region", "shot", "pair"), None, None),
    )
    out_specs = (
        P(("region", "tile"), ("shot", "pair"), None),
        P(("region", "shot", "pair"), "tile", None, None),
        P(("region", "shot", "pair"), "tile", None, None),
    )
    return jax.shard_map(shards, mesh=mesh, in_specs=in_specs, out_specs=out_specs, check_vma=False)
```
